32 devices in a mesh: ctx: 4 (over z), section: 2 (over x), mp: 4 (over y, core).
Axes of the slice: x: 2, y: 2, z: 4, core: 2. Of those that a mesh axis runs over, the one named last changes fastest.
Arguments:
- patches: bfloat16 [2, 768, 3200], P(None, ('ctx', 'mp')), may hold values from -16 to 16
- carried: bfloat16 [768, 3200], P(('ctx', 'mp')), may hold values from -16 to 16
- norm_gain: float32 [2, 3200], P('section'), may hold values from 0.1 to 1.9
- q_gain: float32 [2, 128], P('section'), may hold values from 1.5 to 2.5
- k_gain: float32 [2, 128], P('section'), may hold values from 1.5 to 2.5
- q_weight: bfloat16 [2, 3200, 2048], P('section', None, 'mp'), may hold values from -0.109375 to 0.109375
- k_weight: bfloat16 [2, 3200, 2048], P('section', None, 'mp'), may hold values from -0.109375 to 0.109375
- v_weight: bfloat16 [2, 3200, 2048], P('section', None, 'mp'), may hold values from -0.109375 to 0.109375
- o_weight: bfloat16 [2, 2048, 3200], P('section', 'mp', 'ctx'), may hold values from -0.125 to 0.125
Outputs:
- section_outputs: bfloat16 [2, 2, 768, 3200], P('section', None, ('ctx', 'mp'))
The draws below stay inside these ranges and needn't reach their ends.
All inputs are finite; a program needn't handle non-finite values.
Results may differ from the reference program's by a relative error of at most 0.0063.
Values may be sent and summed in bfloat16 or wider, within the bound.
A program may use at most 128 MiB of HBM per device.

```python
import math
import jax
import jax.numpy as jnp
from jax import lax

D = 3200
HD = 128
HEADS = 16
MICRO = 2
LAYERS = 2
SEQ = 768


def scaled_rows(key, shape):
    first, second, third = jax.random.split(key, 3)
    row_scale = jnp.exp(jax.random.uniform(first, shape[:-1] + (1,), jnp.float32, -1.15, 1.15))
    column_scale = jnp.exp(jax.random.uniform(second, (shape[-1],), jnp.float32, -1.15, 1.15))
    base = jax.random.normal(third, shape, jnp.float32)
    return jnp.clip(base * row_scale * column_scale, -16.0, 16.0)


def draw_patches(key, part):
    return scaled_rows(jax.random.fold_in(key, 11), (MICRO, SEQ, D)).astype(jnp.bfloat16)


def draw_carried(key, part):
    return scaled_rows(jax.random.fold_in(key, 23), (SEQ, D)).astype(jnp.bfloat16)


def block_scale(own_key, dims, cuts, smallest, high):
    loudness = 1.0
    for dim, shards_of in cuts:
        steps = jax.random.uniform(jax.random.fold_in(jax.random.fold_in(own_key, 6), dim), (shards_of,), jnp.float32, smallest / len(cuts), high / len(cuts))
        loudness = loudness * jnp.repeat(jnp.exp(steps), dims[dim] // shards_of).reshape((-1,) + (1,) * (len(dims) - 1 - dim))
    return loudness


def normal_values(own_key, dims, scale, bound, pieces=(), held_as=jnp.bfloat16):
    drawn = jax.random.normal(own_key, dims, jnp.float32) * scale
    if len(pieces) > 0:
        drawn = block_scale(own_key, dims, pieces, -0.22, 0.18) * drawn
    return jnp.clip(drawn, min=-bound, max=bound).astype(held_as)


def setup_inputs(seed: int = 0) -> dict:
    keys = jax.random.split(jax.random.key(seed), 10)
    patches = draw_patches(jax.random.fold_in(keys[9], 71), 0)
    carried = draw_carried(jax.random.fold_in(keys[9], 71), 0)
    norm_gain = jnp.clip(1.0 + 0.18 * jax.random.normal(keys[2], (LAYERS, D), jnp.float32), 0.1, 1.9)
    q_gain = jnp.clip(1.5 + 1.0 * jax.random.uniform(keys[3], (LAYERS, HD), jnp.float32) ** block_scale(keys[3], (LAYERS, HD), ((0, 2),), -0.2, 0.2), 1.5, 2.5)
    k_gain = jnp.clip(1.5 + 1.0 * jax.random.uniform(keys[4], (LAYERS, HD), jnp.float32) ** block_scale(keys[4], (LAYERS, HD), ((0, 2),), -0.2, 0.2), 1.5, 2.5)
    q_weight = normal_values(keys[5], (LAYERS, D, HEADS * HD), D ** -0.5, 0.109375, ((0, 2), (2, 4)))
    k_weight = normal_values(keys[6], (LAYERS, D, HEADS * HD), D ** -0.5, 0.109375, ((0, 2), (2, 4)))
    v_weight = normal_values(keys[7], (LAYERS, D, HEADS * HD), D ** -0.5, 0.109375, ((0, 2), (2, 4)))
    o_weight = normal_values(keys[8], (LAYERS, HEADS * HD, D), (HEADS * HD) ** -0.5, 0.125, ((0, 2), (1, 4), (2, 4)))
    return dict(patches=patches, carried=carried, norm_gain=norm_gain, q_gain=q_gain, k_gain=k_gain, q_weight=q_weight, k_weight=k_weight, v_weight=v_weight, o_weight=o_weight)


epsilon = 1e-06

def rms_scaled(values, gain):
    return values * lax.rsqrt(lax.optimization_barrier(jnp.mean(values * values, axis=-1, keepdims=True)) + epsilon) * gain

def encoder_layer(row_block, layer_gain, query_gain, key_gain, query_weight, key_weight, value_weight, out_weight):
    count = row_block.shape[0]
    head_dim = query_gain.shape[0]
    head_count = query_weight.shape[1] // head_dim
    score_scale = 1.0 / math.sqrt(head_dim)
    normed = rms_scaled(row_block.astype(jnp.float32), layer_gain).astype(jnp.bfloat16)
    raw_query = jnp.dot(normed, query_weight, preferred_element_type=jnp.float32).reshape(count, head_count, head_dim)
    raw_key = jnp.dot(normed, key_weight, preferred_element_type=jnp.float32).reshape(count, head_count, head_dim)
    raw_value = jnp.dot(normed, value_weight, preferred_element_type=jnp.float32).reshape(count, head_count, head_dim)
    queries = rms_scaled(raw_query, query_gain).astype(jnp.bfloat16)
    key_rows = rms_scaled(raw_key, key_gain).astype(jnp.bfloat16)
    value_rows = raw_value.astype(jnp.bfloat16)

    def one_head(operands):
        head_query, head_key, head_value = operands
        scores = jnp.dot(head_query, head_key.T, preferred_element_type=jnp.float32) * score_scale
        probs = jnp.exp(scores)
        totals = lax.optimization_barrier(jnp.sum(probs, axis=1, keepdims=True))
        weighted = jnp.dot(probs.astype(jnp.bfloat16), head_value, preferred_element_type=jnp.float32)
        return weighted / totals
    stacked = lax.map(one_head, (jnp.transpose(queries, (1, 0, 2)), jnp.transpose(key_rows, (1, 0, 2)), jnp.transpose(value_rows, (1, 0, 2))))
    attended = jnp.transpose(stacked, (1, 0, 2)).reshape(count, head_count * head_dim).astype(jnp.bfloat16)
    summed = row_block.astype(jnp.float32) + jnp.dot(attended, out_weight, preferred_element_type=jnp.float32)
    return summed.astype(jnp.bfloat16)

def reference(patches, carried, norm_gain, q_gain, k_gain, q_weight, k_weight, v_weight, o_weight):

    def run_layer(layer, row_block):
        return encoder_layer(row_block, norm_gain[layer], q_gain[layer], k_gain[layer], q_weight[layer], k_weight[layer], v_weight[layer], o_weight[layer])
    first_layer = [run_layer(0, patches[moment]) for moment in range(MICRO)]
    second_layer = [run_layer(1, carried)]
    for moment in range(1, MICRO):
        second_layer.append(run_layer(1, first_layer[moment - 1]))
    return jnp.stack([jnp.stack(first_layer), jnp.stack(second_layer)])
```

```python
import functools
import math

import jax
import jax.numpy as jnp
from jax import lax
from jax.experimental import pallas as pl
from jax.experimental.pallas import tpu as pltpu
from jax.sharding import PartitionSpec as P

epsilon = 1e-06


def rms_scaled(values, gain):
    return values * lax.rsqrt(jnp.mean(values * values, axis=-1, keepdims=True) + epsilon) * gain


def shifted(value, axis, steps):
    count = lax.axis_size(axis)
    leading, last = (max(0, -steps), min(count, count - steps))
    return lax.ppermute(value, axis, [(source, source + steps) for source in range(leading, last)])


def per_device(patches, carried, norm_gain, q_gain, k_gain, q_weight, k_weight, v_weight, o_weight):
    micro_count = patches.shape[0]
    head_dim = q_gain.shape[1]
    head_count = q_weight.shape[2] // head_dim
    columns = head_count * head_dim
    score_scale = 1.0 / math.sqrt(head_dim)
    section_index = lax.axis_index("section")
    incoming = carried
    results = []
    out_weight = lax.all_gather(o_weight[0], "ctx", axis=1, tiled=True)
    for micro_step in range(micro_count):
        layer_input = jnp.where(section_index == 0, patches[micro_step], incoming)
        residual = layer_input.astype(jnp.float32)
        normed = rms_scaled(residual, norm_gain[0]).astype(jnp.bfloat16)
        segment = lax.all_gather(normed, "mp", axis=0, tiled=True)
        rows = segment.shape[0]
        raw_query = jnp.dot(segment, q_weight[0], preferred_element_type=jnp.float32)
        raw_key = jnp.dot(segment, k_weight[0], preferred_element_type=jnp.float32)
        raw_value = jnp.dot(segment, v_weight[0], preferred_element_type=jnp.float32)
        queries = rms_scaled(raw_query.reshape(rows, head_count, head_dim), q_gain[0])
        keys = rms_scaled(raw_key.reshape(rows, head_count, head_dim), k_gain[0])
        keys = keys.astype(jnp.bfloat16).reshape(rows, columns)
        key_block = lax.all_gather(keys, "ctx", axis=0, tiled=True)
        value_block = lax.all_gather(raw_value.astype(jnp.bfloat16), "ctx", axis=0, tiled=True)
        count = key_block.shape[0]
        scores = score_scale * jnp.einsum(
            "qhd,khd->qhk",
            queries.astype(jnp.bfloat16),
            key_block.reshape(count, head_count, head_dim),
            preferred_element_type=jnp.float32,
        )
        probs = jnp.exp(scores)
        totals = jnp.sum(probs, axis=2)
        weighted = jnp.einsum(
            "qhk,khd->qhd",
            probs.astype(jnp.bfloat16),
            value_block.reshape(count, head_count, head_dim),
            preferred_element_type=jnp.float32,
        )
        attended = (weighted / totals[:, :, None]).reshape(rows, columns).astype(jnp.bfloat16)
        partial_value = jnp.dot(attended, out_weight, preferred_element_type=jnp.float32)
        summed = lax.psum_scatter(partial_value, "mp", scatter_dimension=0, tiled=True)
        layer_out = (residual + summed).astype(jnp.bfloat16)
        results.append(layer_out)
        if micro_step + 1 < micro_count:
            incoming = shifted(layer_out, "section", 1)
    return jnp.stack(results)[None]


CHUNKS = 3


class Copies:
    def __init__(self, send_sems, recv_sems):
        self.send_sems, self.recv_sems, self.used = send_sems, recv_sems, 0

    def take(self, count):
        first = self.used
        self.used += count
        return first

    def make(self, index, source, target, device):
        return pltpu.make_async_remote_copy(
            src_ref=source,
            dst_ref=target,
            send_sem=self.send_sems.at[index],
            recv_sem=self.recv_sems.at[index],
            device_id=device,
            device_id_type=pl.DeviceIdType.MESH,
        )


def copies_needed(steps, ctx):
    return steps * (3 * CHUNKS + ctx + ctx * ctx + 3 * ctx) + (steps - 1) * CHUNKS


def layer_kernel(
    steps, ctx,
    patches, carried, norm_gain, q_gain, k_gain, q_weight, k_weight, v_weight, o_weight,
    out,
    xg, normed, wq, wk, wv, wo, heads, qkv, att, pair_out, pair_in, keep, far_out, far_in, fin_out, fin_in, outbuf,
    send_sems, recv_sems, load_sems,
):
    me_ctx = lax.axis_index("ctx")
    me_section = lax.axis_index("section")
    me_mp = lax.axis_index("mp")
    core_peer = {"mp": me_mp + 1 - 2 * lax.rem(me_mp, 2)}
    far_peer = {"mp": lax.rem(me_mp + 2, 4)}
    section_peer = {"section": 1 - me_section}

    def ctx_at(offset):
        return lax.rem(me_ctx + offset + ctx, ctx)

    head_dim = q_gain.shape[1]
    head_count = q_weight.shape[2] // head_dim
    rows = xg.shape[2]
    segment = 4 * rows
    scale = math.log2(math.e) / math.sqrt(head_dim)

    @pl.when(me_section == 0)
    def _():
        for t in range(steps):
            pltpu.make_async_copy(patches.at[t], xg.at[t, 0], load_sems.at[t]).start()

    @pl.when(me_section == 1)
    def _():
        pltpu.make_async_copy(carried, xg.at[0, 0], load_sems.at[0]).start()

    weight_loads = []
    for n, (source, target) in enumerate(((q_weight, wq), (k_weight, wk), (v_weight, wv))):
        weight_loads.append(pltpu.make_async_copy(source.at[0], target, load_sems.at[steps + n]))
    out_loads = []
    for e in range(ctx):
        first = pl.multiple_of(ctx_at(-e) * head_dim, head_dim)
        out_loads.append(
            pltpu.make_async_copy(
                o_weight.at[0, pl.ds(first, head_dim)],
                wo.at[pl.ds(e * head_dim, head_dim)],
                load_sems.at[steps + 3 + e],
            )
        )
    for load in weight_loads + out_loads:
        load.start()

    barrier = pltpu.get_barrier_semaphore()
    peers = [core_peer, far_peer, section_peer] + [{"ctx": ctx_at(d)} for d in range(1, ctx)]
    for peer in peers:
        pl.semaphore_signal(barrier, inc=1, device_id=peer, device_id_type=pl.DeviceIdType.MESH)
    pl.semaphore_wait(barrier, len(peers))

    copies = Copies(send_sems, recv_sems)
    sent = []
    handover = None
    chunk = rows // CHUNKS
    for t in range(steps):
        base = copies.take(3 * CHUNKS)
        near, far, relay = [], [], []
        for i in range(CHUNKS):
            part = pl.ds(i * chunk, chunk)
            far.append(copies.make(base + i, xg.at[t, 0, part], xg.at[t, 2, part], far_peer))
            near.append(copies.make(base + CHUNKS + i, xg.at[t, 0, part], xg.at[t, 1, part], core_peer))
            relay.append(copies.make(base + 2 * CHUNKS + i, xg.at[t, 2, part], xg.at[t, 3, part], core_peer))
        sent += far + near + relay

        if t == 0:
            pltpu.make_async_copy(carried, xg.at[0, 0], load_sems.at[0]).wait()
        else:
            @pl.when(me_section == 0)
            def _():
                pltpu.make_async_copy(patches.at[t], xg.at[t, 0], load_sems.at[t]).wait()

        for i in range(CHUNKS):
            if t > 0:
                incoming = handover[i]

                @pl.when(me_section == 1)
                def _():
                    incoming.wait_recv()

            far[i].start()
            near[i].start()

        def normalize(j):
            values = xg[t, j].astype(jnp.float32)
            normed[pl.ds(j * rows, rows)] = rms_scaled(values, norm_gain[...]).astype(jnp.bfloat16)

        normalize(0)
        for i in range(CHUNKS):
            far[i].wait_recv()
            relay[i].start()
        for i in range(CHUNKS):
            near[i].wait_recv()
        normalize(1)
        normalize(2)
        for i in range(CHUNKS):
            relay[i].wait_recv()
        normalize(3)

        if t == 0:
            for load in weight_loads:
                load.wait()
        base = copies.take(ctx)
        for first in range(0, head_count, 2):
            lanes = pl.ds(first * head_dim, 2 * head_dim)
            raw = [
                jnp.dot(normed[...], w[:, lanes], preferred_element_type=jnp.float32) for w in (wq, wk, wv)
            ]
            for h in (first, first + 1):
                own = slice((h - first) * head_dim, (h - first + 1) * head_dim)
                parts = (
                    rms_scaled(raw[0][:, own], q_gain[...]).astype(jnp.bfloat16),
                    rms_scaled(raw[1][:, own], k_gain[...]).astype(jnp.bfloat16),
                    raw[2][:, own].astype(jnp.bfloat16),
                )

                @pl.when(me_ctx == h)
                def _():
                    for n in range(3):
                        qkv[t, n, 0] = parts[n]

                @pl.when(me_ctx != h)
                def _():
                    for n in range(3):
                        heads[t, h, n] = parts[n]
                    d = lax.rem(h - me_ctx + ctx, ctx)
                    copies.make(base + d, heads.at[t, h], qkv.at[t, :, d], {"ctx": h}).start()

        arrivals = []
        for d in range(1, ctx):
            arrivals.append(copies.make(base + d, heads.at[t, ctx_at(d)], qkv.at[t, :, d], {"ctx": ctx_at(d)}))
        for arrival in arrivals:
            arrival.wait_recv()
        sent += arrivals

        base = copies.take(ctx * ctx)
        keys = qkv[t, 1].reshape(ctx * segment, head_dim)
        vals = qkv[t, 2].reshape(ctx * segment, head_dim)
        gathers = {}
        for d in range(ctx):
            k = (-d) % ctx
            scores = lax.dot_general(
                qkv[t, 0, d], keys, (((1,), (1,)), ((), ())), preferred_element_type=jnp.float32
            )
            probs = jnp.exp2(scores * scale)
            totals = jnp.sum(probs, axis=1, keepdims=True)
            weighted = jnp.dot(probs.astype(jnp.bfloat16), vals, preferred_element_type=jnp.float32)
            att[t, k, 0] = (weighted / totals).astype(jnp.bfloat16)
            for e in range(1, ctx):
                there = (k - e) % ctx
                copy = copies.make(
                    base + there * ctx + e, att.at[t, k, 0], att.at[t, there, e], {"ctx": ctx_at(e)}
                )
                copy.start()
                gathers[there, e] = copy
                sent.append(copy)

        if t == 0:
            for load in out_loads:
                load.wait()
        base = copies.take(3 * ctx)
        pairs, fars, lasts = {}, {}, {}

        def project(k):
            for e in range(1, ctx):
                gathers[k, e].wait_recv()
            lhs = jnp.concatenate([att[t, k, e] for e in range(ctx)], axis=1)
            product = jnp.dot(lhs, wo[...], preferred_element_type=jnp.float32)
            for n in range(2):
                keep[k, n] = product[2 * n * rows:(2 * n + 1) * rows]
                pair_out[t, k, n] = product[(2 * n + 1) * rows:(2 * n + 2) * rows].astype(jnp.bfloat16)
            pairs[k] = copies.make(base + k, pair_out.at[t, k], pair_in.at[t, k], core_peer)
            pairs[k].start()

        def sum_pair(k):
            pairs[k].wait_recv()
            far_out[t, k] = (keep[k, 1] + pair_in[t, k, 1].astype(jnp.float32)).astype(jnp.bfloat16)
            fars[k] = copies.make(base + ctx + k, far_out.at[t, k], far_in.at[t, k], far_peer)
            fars[k].start()
            keep[k, 0] = keep[k, 0] + pair_in[t, k, 0].astype(jnp.float32)

        def sum_far(k):
            fars[k].wait_recv()
            total = (keep[k, 0] + far_in[t, k].astype(jnp.float32)).astype(jnp.bfloat16)
            if k == 0:
                fin_in[t, me_ctx] = total
            else:
                fin_out[t, k] = total
                lasts[k] = copies.make(
                    base + 2 * ctx + k, fin_out.at[t, k], fin_in.at[t, me_ctx], {"ctx": ctx_at(k)}
                )
                lasts[k].start()

        order = list(range(1, ctx)) + [0]
        for n in range(ctx + 3):
            if n < ctx:
                project(order[n])
            if 1 <= n <= ctx:
                sum_pair(order[n - 1])
            if 3 <= n:
                sum_far(order[n - 3])
        sent += list(pairs.values()) + list(fars.values()) + list(lasts.values())
        for k in range(1, ctx):
            copies.make(
                base + 2 * ctx + k, fin_out.at[t, k], fin_in.at[t, ctx_at(-k)], {"ctx": ctx_at(k)}
            ).wait_recv()

        if t + 1 < steps:
            base = copies.take(CHUNKS)
            handover = []
        for i in range(CHUNKS):
            part = pl.ds(i * chunk, chunk)
            summed = jnp.concatenate([fin_in[t, c, part] for c in range(ctx)], axis=1)
            outbuf[t, part] = (xg[t, 0, part].astype(jnp.float32) + summed.astype(jnp.float32)).astype(jnp.bfloat16)
            if t + 1 < steps:
                copy = copies.make(base + i, outbuf.at[t, part], xg.at[t + 1, 0, part], section_peer)
                handover.append(copy)

                @pl.when(me_section == 0)
                def _():
                    copy.start()

        store = pltpu.make_async_copy(outbuf.at[t], out.at[0, t], load_sems.at[steps + 3 + ctx + t])
        store.start()
        if t + 1 == steps:
            for s in range(steps):
                pltpu.make_async_copy(outbuf.at[s], out.at[0, s], load_sems.at[steps + 3 + ctx + s]).wait()
        else:
            handed = handover

            @pl.when(me_section == 0)
            def _():
                for copy in handed:
                    copy.wait_send()

    for copy in sent:
        copy.wait_send()


def fused_device(patches, carried, norm_gain, q_gain, k_gain, q_weight, k_weight, v_weight, o_weight):
    steps, rows, width = patches.shape
    ctx = lax.axis_size("ctx")
    head_dim = q_gain.shape[1]
    columns = q_weight.shape[2]
    share = o_weight.shape[2]
    bf16, f32 = jnp.bfloat16, jnp.float32
    segment = 4 * rows
    anywhere = pl.BlockSpec(memory_space=pl.ANY)
    vmem = pl.BlockSpec(memory_space=pltpu.VMEM)
    number = copies_needed(steps, ctx)
    flops = steps * 2 * segment * (3 * width * columns + ctx * columns * share + 2 * ctx * segment * columns)
    return pl.pallas_call(
        functools.partial(layer_kernel, steps, ctx),
        out_shape=jax.ShapeDtypeStruct((1, steps, rows, width), bf16),
        in_specs=[anywhere, anywhere, vmem, vmem, vmem, anywhere, anywhere, anywhere, anywhere],
        out_specs=anywhere,
        scratch_shapes=[
            pltpu.VMEM((steps, 4, rows, width), bf16),
            pltpu.VMEM((segment, width), bf16),
            pltpu.VMEM((width, columns), bf16),
            pltpu.VMEM((width, columns), bf16),
            pltpu.VMEM((width, columns), bf16),
            pltpu.VMEM((columns, share), bf16),
            pltpu.VMEM((steps, ctx, 3, segment, head_dim), bf16),
            pltpu.VMEM((steps, 3, ctx, segment, head_dim), bf16),
            pltpu.VMEM((steps, ctx, ctx, segment, head_dim), bf16),
            pltpu.VMEM((steps, ctx, 2, rows, share), bf16),
            pltpu.VMEM((steps, ctx, 2, rows, share), bf16),
            pltpu.VMEM((ctx, 2, rows, share), f32),
            pltpu.VMEM((steps, ctx, rows, share), bf16),
            pltpu.VMEM((steps, ctx, rows, share), bf16),
            pltpu.VMEM((steps, ctx, rows, share), bf16),
            pltpu.VMEM((steps, ctx, rows, share), bf16),
            pltpu.VMEM((steps, rows, width), bf16),
            pltpu.SemaphoreType.DMA((number,)),
            pltpu.SemaphoreType.DMA((number,)),
            pltpu.SemaphoreType.DMA((2 * steps + 3 + ctx,)),
        ],
        compiler_params=pltpu.CompilerParams(
            collective_id=0, has_side_effects=True, vmem_limit_bytes=56 * 2**20
        ),
        cost_estimate=pl.CostEstimate(flops=flops, bytes_accessed=12 * 2**20, transcendentals=0),
    )(patches, carried, norm_gain, q_gain, k_gain, q_weight, k_weight, v_weight, o_weight)


def solution(mesh):
    in_specs = (
        P(None, ("ctx", "mp"), None),
        P(("ctx", "mp"), None),
        P("section", None),
        P("section", None),
        P("section", None),
        P("section", None, "mp"),
        P("section", None, "mp"),
        P("section", None, "mp"),
        P("section", "mp", "ctx"),
    )
    out_specs = P("section", None, ("ctx", "mp"), None)

    def program(*arrays):
        ctx, mp, sections = mesh.shape["ctx"], mesh.shape["mp"], mesh.shape["section"]
        heads = arrays[5].shape[2] // arrays[3].shape[1]
        rows = arrays[1].shape[0] // (ctx * mp)
        fits = mp == 4 and sections == 2 and ctx * mp == heads and ctx % 2 == 0 and rows == 16 * CHUNKS
        body = fused_device if fits else per_device
        return jax.shard_map(body, mesh=mesh, in_specs=in_specs, out_specs=out_specs, check_vma=False)(*arrays)

    return program
```

```python
import functools
import math

import jax
import jax.numpy as jnp
from jax import lax
from jax.experimental import pallas as pl
from jax.experimental.pallas import tpu as pltpu
from jax.sharding import PartitionSpec as P

epsilon = 1e-06


def rms_scaled(values, gain):
    return values * lax.rsqrt(jnp.mean(values * values, axis=-1, keepdims=True) + epsilon) * gain


def shifted(value, axis, steps):
    count = lax.axis_size(axis)
    leading, last = (max(0, -steps), min(count, count - steps))
    return lax.ppermute(value, axis, [(source, source + steps) for source in range(leading, last)])


def per_device(patches, carried, norm_gain, q_gain, k_gain, q_weight, k_weight, v_weight, o_weight):
    micro_count = patches.shape[0]
    head_dim = q_gain.shape[1]
    head_count = q_weight.shape[2] // head_dim
    columns = head_count * head_dim
    score_scale = 1.0 / math.sqrt(head_dim)
    section_index = lax.axis_index("section")
    incoming = carried
    results = []
    out_weight = lax.all_gather(o_weight[0], "ctx", axis=1, tiled=True)
    for micro_step in range(micro_count):
        layer_input = jnp.where(section_index == 0, patches[micro_step], incoming)
        residual = layer_input.astype(jnp.float32)
        normed = rms_scaled(residual, norm_gain[0]).astype(jnp.bfloat16)
        segment = lax.all_gather(normed, "mp", axis=0, tiled=True)
        rows = segment.shape[0]
        raw_query = jnp.dot(segment, q_weight[0], preferred_element_type=jnp.float32)
        raw_key = jnp.dot(segment, k_weight[0], preferred_element_type=jnp.float32)
        raw_value = jnp.dot(segment, v_weight[0], preferred_element_type=jnp.float32)
        queries = rms_scaled(raw_query.reshape(rows, head_count, head_dim), q_gain[0])
        keys = rms_scaled(raw_key.reshape(rows, head_count, head_dim), k_gain[0])
        keys = keys.astype(jnp.bfloat16).reshape(rows, columns)
        key_block = lax.all_gather(keys, "ctx", axis=0, tiled=True)
        value_block = lax.all_gather(raw_value.astype(jnp.bfloat16), "ctx", axis=0, tiled=True)
        count = key_block.shape[0]
        scores = score_scale * jnp.einsum(
            "qhd,khd->qhk",
            queries.astype(jnp.bfloat16),
            key_block.reshape(count, head_count, head_dim),
            preferred_element_type=jnp.float32,
        )
        probs = jnp.exp(scores)
        totals = jnp.sum(probs, axis=2)
        weighted = jnp.einsum(
            "qhk,khd->qhd",
            probs.astype(jnp.bfloat16),
            value_block.reshape(count, head_count, head_dim),
            preferred_element_type=jnp.float32,
        )
        attended = (weighted / totals[:, :, None]).reshape(rows, columns).astype(jnp.bfloat16)
        partial_value = jnp.dot(attended, out_weight, preferred_element_type=jnp.float32)
        summed = lax.psum_scatter(partial_value, "mp", scatter_dimension=0, tiled=True)
        layer_out = (residual + summed).astype(jnp.bfloat16)
        results.append(layer_out)
        if micro_step + 1 < micro_count:
            incoming = shifted(layer_out, "section", 1)
    return jnp.stack(results)[None]


CHUNKS = 3


class Copies:
    def __init__(self, send_sems, recv_sems):
        self.send_sems, self.recv_sems, self.used = send_sems, recv_sems, 0

    def take(self, count):
        first = self.used
        self.used += count
        return first

    def make(self, index, source, target, device):
        return pltpu.make_async_remote_copy(
            src_ref=source,
            dst_ref=target,
            send_sem=self.send_sems.at[index],
            recv_sem=self.recv_sems.at[index],
            device_id=device,
            device_id_type=pl.DeviceIdType.MESH,
        )


def copies_needed(steps, ctx):
    return steps * (3 * CHUNKS + 2 * ctx + ctx * ctx + 3 * ctx) + (steps - 1) * CHUNKS


def layer_kernel(
    steps, ctx,
    patches, carried, norm_gain, q_gain, k_gain, q_weight, k_weight, v_weight, o_weight,
    out,
    xg, normed, wq, wk, wv, wo_held, wo, heads, qkv, att, pair_out, pair_in, keep, far_out, far_in, fin_out, fin_in, outbuf,
    send_sems, recv_sems, load_sems,
):
    me_ctx = lax.axis_index("ctx")
    me_section = lax.axis_index("section")
    me_mp = lax.axis_index("mp")
    core_peer = {"mp": me_mp + 1 - 2 * lax.rem(me_mp, 2)}
    far_peer = {"mp": lax.rem(me_mp + 2, 4)}
    section_peer = {"section": 1 - me_section}

    def ctx_at(offset):
        return lax.rem(me_ctx + offset + ctx, ctx)

    def is_direct(offset):
        return me_ctx != (ctx - 1 if offset == 1 else 0)

    head_dim = q_gain.shape[1]
    head_count = q_weight.shape[2] // head_dim
    rows = xg.shape[2]
    segment = 4 * rows
    scale = math.log2(math.e) / math.sqrt(head_dim)

    @pl.when(me_section == 0)
    def _():
        for t in range(steps):
            pltpu.make_async_copy(patches.at[t], xg.at[t, 0], load_sems.at[t]).start()

    @pl.when(me_section == 1)
    def _():
        pltpu.make_async_copy(carried, xg.at[0, 0], load_sems.at[0]).start()

    weight_loads = []
    for n, (source, target) in enumerate(((q_weight, wq), (k_weight, wk), (v_weight, wv))):
        weight_loads.append(pltpu.make_async_copy(source.at[0], target, load_sems.at[steps + n]))
    out_loads = []
    for e in range(ctx):
        first = pl.multiple_of(ctx_at(-e) * head_dim, head_dim)
        out_loads.append(
            pltpu.make_async_copy(
                o_weight.at[0, :, pl.ds(first, head_dim)],
                wo_held.at[e],
                load_sems.at[steps + 3 + e],
            )
        )
    for load in weight_loads + out_loads:
        load.start()

    barrier = pltpu.get_barrier_semaphore()
    peers = [core_peer, far_peer, section_peer] + [{"ctx": ctx_at(d)} for d in range(1, ctx)]
    for peer in peers:
        pl.semaphore_signal(barrier, inc=1, device_id=peer, device_id_type=pl.DeviceIdType.MESH)
    pl.semaphore_wait(barrier, len(peers))

    copies = Copies(send_sems, recv_sems)
    sent, skippable, relays = [], [], []
    handover = None
    chunk = rows // CHUNKS
    for t in range(steps):
        base = copies.take(3 * CHUNKS)
        near, far, relay = [], [], []
        for i in range(CHUNKS):
            part = pl.ds(i * chunk, chunk)
            far.append(copies.make(base + i, xg.at[t, 0, part], xg.at[t, 2, part], far_peer))
            near.append(copies.make(base + CHUNKS + i, xg.at[t, 0, part], xg.at[t, 1, part], core_peer))
            relay.append(copies.make(base + 2 * CHUNKS + i, xg.at[t, 2, part], xg.at[t, 3, part], core_peer))
        sent += far + near + relay

        if t == 0:
            pltpu.make_async_copy(carried, xg.at[0, 0], load_sems.at[0]).wait()
        else:
            @pl.when(me_section == 0)
            def _():
                pltpu.make_async_copy(patches.at[t], xg.at[t, 0], load_sems.at[t]).wait()

        for i in range(CHUNKS):
            if t > 0:
                incoming = handover[i]

                @pl.when(me_section == 1)
                def _():
                    incoming.wait_recv()

            far[i].start()
            near[i].start()

        def normalize(j):
            values = xg[t, j].astype(jnp.float32)
            normed[pl.ds(j * rows, rows)] = rms_scaled(values, norm_gain[...]).astype(jnp.bfloat16)

        normalize(0)
        for i in range(CHUNKS):
            far[i].wait_recv()
            relay[i].start()
        if t == 0:
            for e in range(ctx):
                out_loads[e].wait()
                wo[pl.ds(e * head_dim, head_dim)] = wo_held[e].T
        for i in range(CHUNKS):
            near[i].wait_recv()
        normalize(1)
        normalize(2)
        for i in range(CHUNKS):
            relay[i].wait_recv()
        normalize(3)

        if t == 0:
            for load in weight_loads:
                load.wait()
        base = copies.take(ctx)
        for first in range(0, head_count, 2):
            lanes = pl.ds(first * head_dim, 2 * head_dim)
            raw = [
                jnp.dot(normed[...], w[:, lanes], preferred_element_type=jnp.float32) for w in (wq, wk, wv)
            ]
            for h in (first, first + 1):
                own = slice((h - first) * head_dim, (h - first + 1) * head_dim)
                parts = (
                    rms_scaled(raw[0][:, own], q_gain[...]).astype(jnp.bfloat16),
                    rms_scaled(raw[1][:, own], k_gain[...]).astype(jnp.bfloat16),
                    raw[2][:, own].astype(jnp.bfloat16),
                )

                @pl.when(me_ctx == h)
                def _():
                    for n in range(3):
                        qkv[t, n, 0] = parts[n]

                @pl.when(me_ctx != h)
                def _():
                    for n in range(3):
                        heads[t, h, n] = parts[n]
                    d = lax.rem(h - me_ctx + ctx, ctx)
                    copies.make(base + d, heads.at[t, h], qkv.at[t, :, d], {"ctx": h}).start()

        arrivals = []
        for d in range(1, ctx):
            arrivals.append(copies.make(base + d, heads.at[t, ctx_at(d)], qkv.at[t, :, d], {"ctx": ctx_at(d)}))
        for arrival in arrivals:
            arrival.wait_recv()
        sent += arrivals

        base = gather_base = copies.take(ctx * ctx)
        keys = qkv[t, 1].reshape(ctx * segment, head_dim)
        vals = qkv[t, 2].reshape(ctx * segment, head_dim)
        relay_base = copies.take(ctx)
        gathers = {}
        for d in range(ctx):
            k = (-d) % ctx
            scores = lax.dot_general(
                qkv[t, 0, d], keys, (((1,), (1,)), ((), ())), preferred_element_type=jnp.float32
            )
            probs = jnp.exp2(scores * scale)
            totals = jnp.sum(probs, axis=1, keepdims=True)
            weighted = jnp.dot(probs.astype(jnp.bfloat16), vals, preferred_element_type=jnp.float32)
            att[t, k, 0] = (weighted / totals).astype(jnp.bfloat16)
            for e in range(1, ctx):
                there = (k - e) % ctx
                copy = copies.make(
                    base + there * ctx + e, att.at[t, k, 0], att.at[t, there, e], {"ctx": ctx_at(e)}
                )
                gathers[there, e] = copy
                if e in (1, ctx - 1):
                    @pl.when(is_direct(e))
                    def _():
                        copy.start()

                    skippable.append((e, copy))
                else:
                    copy.start()
                    sent.append(copy)

        base = copies.take(3 * ctx)
        pairs, fars, lasts = {}, {}, {}

        def relay_ends(k):
            gathers[k, 2].wait_recv()
            for r, to, e in ((1, 0, 1), (ctx - 2, ctx - 1, ctx - 1)):
                there = (k + r - to) % ctx
                copy = pltpu.make_async_remote_copy(
                    src_ref=att.at[t, k, 2],
                    dst_ref=att.at[t, there, e],
                    send_sem=copies.send_sems.at[relay_base + k],
                    recv_sem=copies.recv_sems.at[gather_base + there * ctx + e],
                    device_id={"ctx": to},
                    device_id_type=pl.DeviceIdType.MESH,
                )
                relays.append((r, copy))

                @pl.when(me_ctx == r)
                def _():
                    copy.start()

        def project(k):
            for e in range(1, ctx):
                if e != 2:
                    gathers[k, e].wait_recv()
            lhs = jnp.concatenate([att[t, k, e] for e in range(ctx)], axis=1)
            product = jnp.dot(lhs, wo[...], preferred_element_type=jnp.float32)
            for n in range(2):
                keep[k, n] = product[2 * n * rows:(2 * n + 1) * rows]
                pair_out[t, k, n] = product[(2 * n + 1) * rows:(2 * n + 2) * rows].astype(jnp.bfloat16)
            pairs[k] = copies.make(base + k, pair_out.at[t, k], pair_in.at[t, k], core_peer)
            pairs[k].start()

        def sum_pair(k):
            pairs[k].wait_recv()
            far_out[t, k] = (keep[k, 1] + pair_in[t, k, 1].astype(jnp.float32)).astype(jnp.bfloat16)
            fars[k] = copies.make(base + ctx + k, far_out.at[t, k], far_in.at[t, k], far_peer)
            fars[k].start()
            keep[k, 0] = keep[k, 0] + pair_in[t, k, 0].astype(jnp.float32)

        def sum_far(k):
            fars[k].wait_recv()
            total = (keep[k, 0] + far_in[t, k].astype(jnp.float32)).astype(jnp.bfloat16)
            if k == 0:
                fin_in[t, me_ctx] = total
            else:
                fin_out[t, k] = total
                lasts[k] = copies.make(
                    base + 2 * ctx + k, fin_out.at[t, k], fin_in.at[t, me_ctx], {"ctx": ctx_at(k)}
                )
                lasts[k].start()

        order = list(range(1, ctx)) + [0]
        relay_ends(2)
        relay_ends(1)
        for n in range(ctx + 3):
            if n < ctx:
                project(order[n])
            if n < 2:
                relay_ends((0, 3)[n])
            if 1 <= n <= ctx:
                sum_pair(order[n - 1])
            if 3 <= n:
                sum_far(order[n - 3])
        sent += list(pairs.values()) + list(fars.values()) + list(lasts.values())
        for k in range(1, ctx):
            copies.make(
                base + 2 * ctx + k, fin_out.at[t, k], fin_in.at[t, ctx_at(-k)], {"ctx": ctx_at(k)}
            ).wait_recv()

        if t + 1 < steps:
            base = copies.take(CHUNKS)
            handover = []
        for i in range(CHUNKS):
            part = pl.ds(i * chunk, chunk)
            summed = jnp.concatenate([fin_in[t, c, part] for c in range(ctx)], axis=1)
            outbuf[t, part] = (xg[t, 0, part].astype(jnp.float32) + summed.astype(jnp.float32)).astype(jnp.bfloat16)
            if t + 1 < steps:
                copy = copies.make(base + i, outbuf.at[t, part], xg.at[t + 1, 0, part], section_peer)
                handover.append(copy)

                @pl.when(me_section == 0)
                def _():
                    copy.start()

        store = pltpu.make_async_copy(outbuf.at[t], out.at[0, t], load_sems.at[steps + 3 + ctx + t])
        store.start()
        if t + 1 == steps:
            for s in range(steps):
                pltpu.make_async_copy(outbuf.at[s], out.at[0, s], load_sems.at[steps + 3 + ctx + s]).wait()
        else:
            handed = handover

            @pl.when(me_section == 0)
            def _():
                for copy in handed:
                    copy.wait_send()

    for copy in sent:
        copy.wait_send()
    for e, copy in skippable:
        @pl.when(is_direct(e))
        def _():
            copy.wait_send()

    for r, copy in relays:
        @pl.when(me_ctx == r)
        def _():
            copy.wait_send()


def fused_device(patches, carried, norm_gain, q_gain, k_gain, q_weight, k_weight, v_weight, o_weight):
    steps, rows, width = patches.shape
    ctx = lax.axis_size("ctx")
    head_dim = q_gain.shape[1]
    columns = q_weight.shape[2]
    share = o_weight.shape[2]
    bf16, f32 = jnp.bfloat16, jnp.float32
    segment = 4 * rows
    anywhere = pl.BlockSpec(memory_space=pl.ANY)
    vmem = pl.BlockSpec(memory_space=pltpu.VMEM)
    number = copies_needed(steps, ctx)
    flops = steps * 2 * segment * (3 * width * columns + ctx * columns * share + 2 * ctx * segment * columns)
    return pl.pallas_call(
        functools.partial(layer_kernel, steps, ctx),
        out_shape=jax.ShapeDtypeStruct((1, steps, rows, width), bf16),
        in_specs=[anywhere, anywhere, vmem, vmem, vmem, anywhere, anywhere, anywhere, anywhere],
        out_specs=anywhere,
        scratch_shapes=[
            pltpu.VMEM((steps, 4, rows, width), bf16),
            pltpu.VMEM((segment, width), bf16),
            pltpu.VMEM((width, columns), bf16),
            pltpu.VMEM((width, columns), bf16),
            pltpu.VMEM((width, columns), bf16),
            pltpu.VMEM((ctx, share, head_dim), bf16),
            pltpu.VMEM((columns, share), bf16),
            pltpu.VMEM((steps, ctx, 3, segment, head_dim), bf16),
            pltpu.VMEM((steps, 3, ctx, segment, head_dim), bf16),
            pltpu.VMEM((steps, ctx, ctx, segment, head_dim), bf16),
            pltpu.VMEM((steps, ctx, 2, rows, share), bf16),
            pltpu.VMEM((steps, ctx, 2, rows, share), bf16),
            pltpu.VMEM((ctx, 2, rows, share), f32),
            pltpu.VMEM((steps, ctx, rows, share), bf16),
            pltpu.VMEM((steps, ctx, rows, share), bf16),
            pltpu.VMEM((steps, ctx, rows, share), bf16),
            pltpu.VMEM((steps, ctx, rows, share), bf16),
            pltpu.VMEM((steps, rows, width), bf16),
            pltpu.SemaphoreType.DMA((number,)),
            pltpu.SemaphoreType.DMA((number,)),
            pltpu.SemaphoreType.DMA((2 * steps + 3 + ctx,)),
        ],
        compiler_params=pltpu.CompilerParams(
            collective_id=0, has_side_effects=True, vmem_limit_bytes=56 * 2**20
        ),
        cost_estimate=pl.CostEstimate(flops=flops, bytes_accessed=12 * 2**20, transcendentals=0),
    )(patches, carried, norm_gain, q_gain, k_gain, q_weight, k_weight, v_weight, jnp.swapaxes(o_weight, 1, 2))


def solution(mesh):
    in_specs = (
        P(None, ("ctx", "mp"), None),
        P(("ctx", "mp"), None),
        P("section", None),
        P("section", None),
        P("section", None),
        P("section", None, "mp"),
        P("section", None, "mp"),
        P("section", None, "mp"),
        P("section", "mp", "ctx"),
    )
    out_specs = P("section", None, ("ctx", "mp"), None)

    def program(*arrays):
        ctx, mp, sections = mesh.shape["ctx"], mesh.shape["mp"], mesh.shape["section"]
        heads = arrays[5].shape[2] // arrays[3].shape[1]
        rows = arrays[1].shape[0] // (ctx * mp)
        fits = mp == 4 and sections == 2 and ctx * mp == heads and ctx == 4 and rows == 16 * CHUNKS
        body = fused_device if fits else per_device
        return jax.shard_map(body, mesh=mesh, in_specs=in_specs, out_specs=out_specs, check_vma=False)(*arrays)

    return program
```

```python
import functools
import math

import jax
import jax.numpy as jnp
from jax import lax
from jax.experimental import pallas as pl
from jax.experimental.pallas import tpu as pltpu
from jax.sharding import PartitionSpec as P

epsilon = 1e-06


def rms_scaled(values, gain):
    return values * lax.rsqrt(jnp.mean(values * values, axis=-1, keepdims=True) + epsilon) * gain


def shifted(value, axis, steps):
    count = lax.axis_size(axis)
    leading, last = (max(0, -steps), min(count, count - steps))
    return lax.ppermute(value, axis, [(source, source + steps) for source in range(leading, last)])


def per_device(patches, carried, norm_gain, q_gain, k_gain, q_weight, k_weight, v_weight, o_weight):
    micro_count = patches.shape[0]
    head_dim = q_gain.shape[1]
    head_count = q_weight.shape[2] // head_dim
    columns = head_count * head_dim
    score_scale = 1.0 / math.sqrt(head_dim)
    section_index = lax.axis_index("section")
    incoming = carried
    results = []
    out_weight = lax.all_gather(o_weight[0], "ctx", axis=1, tiled=True)
    for micro_step in range(micro_count):
        layer_input = jnp.where(section_index == 0, patches[micro_step], incoming)
        residual = layer_input.astype(jnp.float32)
        normed = rms_scaled(residual, norm_gain[0]).astype(jnp.bfloat16)
        segment = lax.all_gather(normed, "mp", axis=0, tiled=True)
        rows = segment.shape[0]
        raw_query = jnp.dot(segment, q_weight[0], preferred_element_type=jnp.float32)
        raw_key = jnp.dot(segment, k_weight[0], preferred_element_type=jnp.float32)
        raw_value = jnp.dot(segment, v_weight[0], preferred_element_type=jnp.float32)
        queries = rms_scaled(raw_query.reshape(rows, head_count, head_dim), q_gain[0])
        keys = rms_scaled(raw_key.reshape(rows, head_count, head_dim), k_gain[0])
        keys = keys.astype(jnp.bfloat16).reshape(rows, columns)
        key_block = lax.all_gather(keys, "ctx", axis=0, tiled=True)
        value_block = lax.all_gather(raw_value.astype(jnp.bfloat16), "ctx", axis=0, tiled=True)
        count = key_block.shape[0]
        scores = score_scale * jnp.einsum(
            "qhd,khd->qhk",
            queries.astype(jnp.bfloat16),
            key_block.reshape(count, head_count, head_dim),
            preferred_element_type=jnp.float32,
        )
        probs = jnp.exp(scores)
        totals = jnp.sum(probs, axis=2)
        weighted = jnp.einsum(
            "qhk,khd->qhd",
            probs.astype(jnp.bfloat16),
            value_block.reshape(count, head_count, head_dim),
            preferred_element_type=jnp.float32,
        )
        attended = (weighted / totals[:, :, None]).reshape(rows, columns).astype(jnp.bfloat16)
        partial_value = jnp.dot(attended, out_weight, preferred_element_type=jnp.float32)
        summed = lax.psum_scatter(partial_value, "mp", scatter_dimension=0, tiled=True)
        layer_out = (residual + summed).astype(jnp.bfloat16)
        results.append(layer_out)
        if micro_step + 1 < micro_count:
            incoming = shifted(layer_out, "section", 1)
    return jnp.stack(results)[None]


CHUNKS = 3


class Copies:
    def __init__(self, send_sems, recv_sems):
        self.send_sems, self.recv_sems, self.used = send_sems, recv_sems, 0

    def take(self, count):
        first = self.used
        self.used += count
        return first

    def make(self, index, source, target, device):
        return pltpu.make_async_remote_copy(
            src_ref=source,
            dst_ref=target,
            send_sem=self.send_sems.at[index],
            recv_sem=self.recv_sems.at[index],
            device_id=device,
            device_id_type=pl.DeviceIdType.MESH,
        )


def copies_needed(steps, ctx):
    return steps * (3 * CHUNKS + 2 * ctx + ctx * ctx + 3 * ctx) + (steps - 1) * CHUNKS


def layer_kernel(
    steps, ctx,
    patches, carried, norm_gain, q_gain, k_gain, q_weight, k_weight, v_weight, o_weight,
    out,
    xg, normed, wq, wk, wv, wo_held, wo, heads, qkv, att, pair_out, pair_in, keep, far_out, far_in, fin_out, fin_in, outbuf,
    send_sems, recv_sems, load_sems,
):
    me_ctx = lax.axis_index("ctx")
    me_section = lax.axis_index("section")
    me_mp = lax.axis_index("mp")
    core_peer = {"mp": me_mp + 1 - 2 * lax.rem(me_mp, 2)}
    far_peer = {"mp": lax.rem(me_mp + 2, 4)}
    section_peer = {"section": 1 - me_section}

    def ctx_at(offset):
        return lax.rem(me_ctx + offset + ctx, ctx)

    def is_direct(offset):
        return me_ctx != (ctx - 1 if offset == 1 else 0)

    head_dim = q_gain.shape[1]
    head_count = q_weight.shape[2] // head_dim
    rows = xg.shape[2]
    segment = 4 * rows
    scale = math.log2(math.e) / math.sqrt(head_dim)

    @pl.when(me_section == 0)
    def _():
        for t in range(steps):
            pltpu.make_async_copy(patches.at[t], xg.at[t, 0], load_sems.at[t]).start()

    @pl.when(me_section == 1)
    def _():
        pltpu.make_async_copy(carried, xg.at[0, 0], load_sems.at[0]).start()

    head_order = [h for n in range(head_count // 2) for h in (n, head_count - 1 - n)]
    weight_loads = []
    for n, (source, target) in enumerate(((q_weight, wq), (k_weight, wk), (v_weight, wv))):
        for place, h in enumerate(head_order):
            weight_loads.append(
                pltpu.make_async_copy(
                    source.at[0, :, pl.ds(h * head_dim, head_dim)],
                    target.at[:, pl.ds(place * head_dim, head_dim)],
                    load_sems.at[2 * steps + 3 + ctx + n * head_count + place],
                )
            )
    out_loads = []
    for e in range(ctx):
        first = pl.multiple_of(ctx_at(-e) * head_dim, head_dim)
        out_loads.append(
            pltpu.make_async_copy(
                o_weight.at[0, :, pl.ds(first, head_dim)],
                wo_held.at[e],
                load_sems.at[steps + 3 + e],
            )
        )
    for load in weight_loads + out_loads:
        load.start()

    barrier = pltpu.get_barrier_semaphore()
    peers = [core_peer, far_peer, section_peer] + [{"ctx": ctx_at(d)} for d in range(1, ctx)]
    for peer in peers:
        pl.semaphore_signal(barrier, inc=1, device_id=peer, device_id_type=pl.DeviceIdType.MESH)
    pl.semaphore_wait(barrier, len(peers))

    copies = Copies(send_sems, recv_sems)
    sent, skippable, relays = [], [], []
    handover = None
    chunk = rows // CHUNKS
    for t in range(steps):
        base = copies.take(3 * CHUNKS)
        near, far, relay = [], [], []
        for i in range(CHUNKS):
            part = pl.ds(i * chunk, chunk)
            far.append(copies.make(base + i, xg.at[t, 0, part], xg.at[t, 2, part], far_peer))
            near.append(copies.make(base + CHUNKS + i, xg.at[t, 0, part], xg.at[t, 1, part], core_peer))
            relay.append(copies.make(base + 2 * CHUNKS + i, xg.at[t, 2, part], xg.at[t, 3, part], core_peer))
        sent += far + near + relay

        if t == 0:
            pltpu.make_async_copy(carried, xg.at[0, 0], load_sems.at[0]).wait()
        else:
            @pl.when(me_section == 0)
            def _():
                pltpu.make_async_copy(patches.at[t], xg.at[t, 0], load_sems.at[t]).wait()

        for i in range(CHUNKS):
            if t > 0:
                incoming = handover[i]

                @pl.when(me_section == 1)
                def _():
                    incoming.wait_recv()

            far[i].start()
            near[i].start()

        def normalize(j):
            values = xg[t, j].astype(jnp.float32)
            normed[pl.ds(j * rows, rows)] = rms_scaled(values, norm_gain[...]).astype(jnp.bfloat16)

        normalize(0)
        for i in range(CHUNKS):
            far[i].wait_recv()
            relay[i].start()
        if t == 0:
            for e in range(ctx):
                out_loads[e].wait()
                wo[pl.ds(e * head_dim, head_dim)] = wo_held[e].T
        for i in range(CHUNKS):
            near[i].wait_recv()
        normalize(1)
        normalize(2)
        for i in range(CHUNKS):
            relay[i].wait_recv()
        normalize(3)

        if t == 0:
            for load in weight_loads:
                load.wait()
        base = copies.take(ctx)
        for first in range(0, head_count, 2):
            lanes = pl.ds(first * head_dim, 2 * head_dim)
            raw = [
                jnp.dot(normed[...], w[:, lanes], preferred_element_type=jnp.float32) for w in (wq, wk, wv)
            ]
            for side in range(2):
                h = head_order[first + side]
                own = slice(side * head_dim, (side + 1) * head_dim)
                parts = (
                    rms_scaled(raw[0][:, own], q_gain[...]).astype(jnp.bfloat16),
                    rms_scaled(raw[1][:, own], k_gain[...]).astype(jnp.bfloat16),
                    raw[2][:, own].astype(jnp.bfloat16),
                )

                @pl.when(me_ctx == h)
                def _():
                    for n in range(3):
                        qkv[t, n, 0] = parts[n]

                @pl.when(me_ctx != h)
                def _():
                    for n in range(3):
                        heads[t, h, n] = parts[n]
                    d = lax.rem(h - me_ctx + ctx, ctx)
                    copies.make(base + d, heads.at[t, h], qkv.at[t, :, d], {"ctx": h}).start()

        arrivals = []
        for d in range(1, ctx):
            arrivals.append(copies.make(base + d, heads.at[t, ctx_at(d)], qkv.at[t, :, d], {"ctx": ctx_at(d)}))
        for arrival in arrivals:
            arrival.wait_recv()
        sent += arrivals

        base = gather_base = copies.take(ctx * ctx)
        keys = qkv[t, 1].reshape(ctx * segment, head_dim)
        vals = qkv[t, 2].reshape(ctx * segment, head_dim)
        relay_base = copies.take(ctx)
        gathers = {}
        for d in range(ctx):
            k = (-d) % ctx
            scores = lax.dot_general(
                qkv[t, 0, d], keys, (((1,), (1,)), ((), ())), preferred_element_type=jnp.float32
            )
            probs = jnp.exp2(scores * scale)
            totals = jnp.sum(probs, axis=1, keepdims=True)
            weighted = jnp.dot(probs.astype(jnp.bfloat16), vals, preferred_element_type=jnp.float32)
            att[t, k, 0] = (weighted / totals).astype(jnp.bfloat16)
            for e in range(1, ctx):
                there = (k - e) % ctx
                copy = copies.make(
                    base + there * ctx + e, att.at[t, k, 0], att.at[t, there, e], {"ctx": ctx_at(e)}
                )
                gathers[there, e] = copy
                if e in (1, ctx - 1):
                    @pl.when(is_direct(e))
                    def _():
                        copy.start()

                    skippable.append((e, copy))
                else:
                    copy.start()
                    sent.append(copy)

        base = copies.take(3 * ctx)
        pairs, fars, lasts = {}, {}, {}

        def relay_ends(k):
            gathers[k, 2].wait_recv()
            for r, to, e in ((1, 0, 1), (ctx - 2, ctx - 1, ctx - 1)):
                there = (k + r - to) % ctx
                copy = pltpu.make_async_remote_copy(
                    src_ref=att.at[t, k, 2],
                    dst_ref=att.at[t, there, e],
                    send_sem=copies.send_sems.at[relay_base + k],
                    recv_sem=copies.recv_sems.at[gather_base + there * ctx + e],
                    device_id={"ctx": to},
                    device_id_type=pl.DeviceIdType.MESH,
                )
                relays.append((r, copy))

                @pl.when(me_ctx == r)
                def _():
                    copy.start()

        def project(k):
            for e in range(1, ctx):
                if e != 2:
                    gathers[k, e].wait_recv()
            lhs = jnp.concatenate([att[t, k, e] for e in range(ctx)], axis=1)
            product = jnp.dot(lhs, wo[...], preferred_element_type=jnp.float32)
            for n in range(2):
                keep[k, n] = product[2 * n * rows:(2 * n + 1) * rows]
                pair_out[t, k, n] = product[(2 * n + 1) * rows:(2 * n + 2) * rows].astype(jnp.bfloat16)
            pairs[k] = copies.make(base + k, pair_out.at[t, k], pair_in.at[t, k], core_peer)
            pairs[k].start()

        def sum_pair(k):
            pairs[k].wait_recv()
            far_out[t, k] = (keep[k, 1] + pair_in[t, k, 1].astype(jnp.float32)).astype(jnp.bfloat16)
            fars[k] = copies.make(base + ctx + k, far_out.at[t, k], far_in.at[t, k], far_peer)
            fars[k].start()
            keep[k, 0] = keep[k, 0] + pair_in[t, k, 0].astype(jnp.float32)

        def sum_far(k):
            fars[k].wait_recv()
            total = (keep[k, 0] + far_in[t, k].astype(jnp.float32)).astype(jnp.bfloat16)
            if k == 0:
                fin_in[t, me_ctx] = total
            else:
                fin_out[t, k] = total
                lasts[k] = copies.make(
                    base + 2 * ctx + k, fin_out.at[t, k], fin_in.at[t, me_ctx], {"ctx": ctx_at(k)}
                )
                lasts[k].start()

        order = list(range(1, ctx)) + [0]
        relay_ends(2)
        relay_ends(1)
        for n in range(ctx + 3):
            if n < ctx:
                project(order[n])
            if n < 2:
                relay_ends((0, 3)[n])
            if 1 <= n <= ctx:
                sum_pair(order[n - 1])
            if 3 <= n:
                sum_far(order[n - 3])
        sent += list(pairs.values()) + list(fars.values()) + list(lasts.values())
        for k in range(1, ctx):
            copies.make(
                base + 2 * ctx + k, fin_out.at[t, k], fin_in.at[t, ctx_at(-k)], {"ctx": ctx_at(k)}
            ).wait_recv()

        if t + 1 < steps:
            base = copies.take(CHUNKS)
            handover = []
        for i in range(CHUNKS):
            part = pl.ds(i * chunk, chunk)
            summed = jnp.concatenate([fin_in[t, c, part] for c in range(ctx)], axis=1)
            outbuf[t, part] = (xg[t, 0, part].astype(jnp.float32) + summed.astype(jnp.float32)).astype(jnp.bfloat16)
            if t + 1 < steps:
                copy = copies.make(base + i, outbuf.at[t, part], xg.at[t + 1, 0, part], section_peer)
                handover.append(copy)

                @pl.when(me_section == 0)
                def _():
                    copy.start()

        store = pltpu.make_async_copy(outbuf.at[t], out.at[0, t], load_sems.at[steps + 3 + ctx + t])
        store.start()
        if t + 1 == steps:
            for s in range(steps):
                pltpu.make_async_copy(outbuf.at[s], out.at[0, s], load_sems.at[steps + 3 + ctx + s]).wait()
        else:
            handed = handover

            @pl.when(me_section == 0)
            def _():
                for copy in handed:
                    copy.wait_send()

    for copy in sent:
        copy.wait_send()
    for e, copy in skippable:
        @pl.when(is_direct(e))
        def _():
            copy.wait_send()

    for r, copy in relays:
        @pl.when(me_ctx == r)
        def _():
            copy.wait_send()


def fused_device(patches, carried, norm_gain, q_gain, k_gain, q_weight, k_weight, v_weight, o_weight):
    steps, rows, width = patches.shape
    ctx = lax.axis_size("ctx")
    head_dim = q_gain.shape[1]
    columns = q_weight.shape[2]
    share = o_weight.shape[2]
    bf16, f32 = jnp.bfloat16, jnp.float32
    segment = 4 * rows
    anywhere = pl.BlockSpec(memory_space=pl.ANY)
    vmem = pl.BlockSpec(memory_space=pltpu.VMEM)
    number = copies_needed(steps, ctx)
    flops = steps * 2 * segment * (3 * width * columns + ctx * columns * share + 2 * ctx * segment * columns)
    return pl.pallas_call(
        functools.partial(layer_kernel, steps, ctx),
        out_shape=jax.ShapeDtypeStruct((1, steps, rows, width), bf16),
        in_specs=[anywhere, anywhere, vmem, vmem, vmem, anywhere, anywhere, anywhere, anywhere],
        out_specs=anywhere,
        scratch_shapes=[
            pltpu.VMEM((steps, 4, rows, width), bf16),
            pltpu.VMEM((segment, width), bf16),
            pltpu.VMEM((width, columns), bf16),
            pltpu.VMEM((width, columns), bf16),
            pltpu.VMEM((width, columns), bf16),
            pltpu.VMEM((ctx, share, head_dim), bf16),
            pltpu.VMEM((columns, share), bf16),
            pltpu.VMEM((steps, ctx, 3, segment, head_dim), bf16),
            pltpu.VMEM((steps, 3, ctx, segment, head_dim), bf16),
            pltpu.VMEM((steps, ctx, ctx, segment, head_dim), bf16),
            pltpu.VMEM((steps, ctx, 2, rows, share), bf16),
            pltpu.VMEM((steps, ctx, 2, rows, share), bf16),
            pltpu.VMEM((ctx, 2, rows, share), f32),
            pltpu.VMEM((steps, ctx, rows, share), bf16),
            pltpu.VMEM((steps, ctx, rows, share), bf16),
            pltpu.VMEM((steps, ctx, rows, share), bf16),
            pltpu.VMEM((steps, ctx, rows, share), bf16),
            pltpu.VMEM((steps, rows, width), bf16),
            pltpu.SemaphoreType.DMA((number,)),
            pltpu.SemaphoreType.DMA((number,)),
            pltpu.SemaphoreType.DMA((2 * steps + 3 + ctx + 3 * (columns // head_dim),)),
        ],
        compiler_params=pltpu.CompilerParams(
            collective_id=0, has_side_effects=True, vmem_limit_bytes=56 * 2**20
        ),
        cost_estimate=pl.CostEstimate(flops=flops, bytes_accessed=12 * 2**20, transcendentals=0),
    )(patches, carried, norm_gain, q_gain, k_gain, q_weight, k_weight, v_weight, jnp.swapaxes(o_weight, 1, 2))


def solution(mesh):
    in_specs = (
        P(None, ("ctx", "mp"), None),
        P(("ctx", "mp"), None),
        P("section", None),
        P("section", None),
        P("section", None),
        P("section", None, "mp"),
        P("section", None, "mp"),
        P("section", None, "mp"),
        P("section", "mp", "ctx"),
    )
    out_specs = P("section", None, ("ctx", "mp"), None)

    def program(*arrays):
        ctx, mp, sections = mesh.shape["ctx"], mesh.shape["mp"], mesh.shape["section"]
        heads = arrays[5].shape[2] // arrays[3].shape[1]
        rows = arrays[1].shape[0] // (ctx * mp)
        fits = mp == 4 and sections == 2 and ctx * mp == heads and ctx == 4 and rows == 16 * CHUNKS
        body = fused_device if fits else per_device
        return jax.shard_map(body, mesh=mesh, in_specs=in_specs, out_specs=out_specs, check_vma=False)(*arrays)

    return program
```
